128 devices in a mesh: grp: 8 (over z_lo, x), shard: 16 (over y, z_hi, core).
Axes of the slice: x: 4, y: 4, z: 4 (z_hi: 2, z_lo: 2; z = z_hi * 2 + z_lo), core: 2. Of those that a mesh axis runs over, the one named last changes fastest.
Arguments:
- amplitudes: float32 [1024, 65536], P(None, 'shard'), may hold values from -6 to 6
- integrals: float32 [8192, 65536], P('grp', 'shard'), may hold values from -0.0234375 to 0.0234375
- cycle_inter: float32 [8192, 8192], P('shard', 'grp'), may hold values from -0.0625 to 0.0625
Outputs:
- cycle_out: float32 [1024, 8192], P('shard', 'grp')
The draws below stay inside these ranges and needn't reach their ends.
All inputs are finite; a program needn't handle non-finite values.
Results may differ from the reference program's by a relative error of at most 0.000076.
Values sent between devices are 32-bit elements; how exact they have to be, the bound alone decides.
No kernel may reach another device: no remote copies, remote signals or barrier semaphores. Data moves between devices by JAX's collectives and lax.ppermute only.
A program may use at most 128 MiB of HBM per device.

```python
import jax
import jax.numpy as jnp
from jax import lax

O = 32
A = 32
C = 256
EF = 65536
OO = 1024
AC = 8192
CK = 8192
BJ = 8192


def shard_levels(rng, extent, split, low, top_value):
    level, own = 1.0, jax.random.fold_in(rng, 6)
    for axis_at, shards_of in split:
        draws = jnp.exp(jax.random.uniform(jax.random.fold_in(own, axis_at), (shards_of,), jnp.float32, low / len(split), top_value / len(split)))
        level = level * jnp.repeat(draws, extent[axis_at] // shards_of).reshape([-1 if axis == axis_at else 1 for axis in range(len(extent))])
    return level


def gaussian(key, shape, deviation, most, shards=(), kind=jnp.bfloat16):
    entries = jax.random.normal(key, shape, jnp.float32) * deviation
    if len(shards) > 0:
        entries = shard_levels(key, shape, shards, -0.22, 0.18) * entries
    return jnp.clip(entries, min=-most, max=most).astype(kind)


def setup_inputs(seed: int = 0) -> dict:
    keys = jax.random.split(jax.random.key(seed), 4)
    amplitudes = gaussian(keys[0], (OO, EF), 1.0, 6.0, ((1, 16),), jnp.float32)
    integrals = gaussian(keys[1], (AC, EF), EF ** -0.5, 0.0234375, ((0, 8), (1, 16)), jnp.float32)
    cycle_inter = gaussian(keys[2], (CK, BJ), CK ** -0.5, 0.0625, ((0, 16), (1, 8)), jnp.float32)
    return {"amplitudes": amplitudes, "integrals": integrals, "cycle_inter": cycle_inter}


def reference(amplitudes, integrals, cycle_inter):
    ladder = jnp.dot(amplitudes, integrals.T, preferred_element_type=jnp.float32, precision=lax.Precision.HIGHEST)
    regrouped = ladder.reshape(O, O, A, C).transpose(2, 0, 3, 1).reshape(A * O, C * O)
    return jnp.dot(regrouped, cycle_inter, preferred_element_type=jnp.float32, precision=lax.Precision.HIGHEST)
```

```python
import jax
import jax.numpy as jnp
from jax import lax
from jax.sharding import Mesh, PartitionSpec as P

AXES = ("zl", "x", "y", "zh", "c")
C = 256
O = 32
MODE = "direct"
CHUNKS = ((0, 0, 32), (1, 0, 32))
SWAP = ((0, 1), (1, 0))


def dot(a, b, dims):
    return lax.dot_general(
        a, b, (dims, ((), ())), precision=lax.Precision.HIGH, preferred_element_type=jnp.float32
    )


def pick(x, index):
    return lax.dynamic_index_in_dim(x, index, 0, keepdims=False)


def scatter_sum(x):
    if MODE == "direct":
        got = lax.all_to_all(x.reshape((8,) + x.shape[2:]), ("y", "zh"), 0, 0)
        return jnp.sum(got, 0)
    got = jnp.sum(lax.all_to_all(x, "y", 0, 0), 0)
    zh = lax.axis_index("zh")
    return pick(got, zh) + lax.ppermute(pick(got, 1 - zh), "zh", SWAP)


def spread(x):
    if MODE == "direct":
        return lax.all_to_all(jnp.broadcast_to(x[None], (8,) + x.shape), ("zl", "x"), 0, 0)
    both = lax.all_to_all(jnp.broadcast_to(x[None], (2,) + x.shape), "zl", 0, 0)
    every = lax.all_to_all(jnp.broadcast_to(both[None], (4,) + both.shape), "x", 0, 0)
    return every.swapaxes(0, 1).reshape((8,) + x.shape)


def shards(amplitudes, integrals, cycle_inter):
    core = lax.axis_index("c")
    ef = amplitudes.shape[1]
    slab = integrals.reshape(2, 2, C, ef)
    other = lax.ppermute(cycle_inter, "c", SWAP)
    outs = {0: [], 1: []}
    for h, lo, hi in CHUNKS:
        n = hi - lo
        block = dot(
            slab[:, h].reshape(2 * C, ef), amplitudes[lo * O : hi * O], ((1,), (1,))
        ).reshape(2, C, n * O)
        mine = pick(block, core) + lax.ppermute(pick(block, 1 - core), "c", SWAP)
        summed = scatter_sum(mine.reshape(4, 2, C // 8, n * O))
        pair = summed.reshape(2, C // 16, n, O).transpose(0, 2, 1, 3).reshape(2, n, C // 16 * O)
        rows = spread(pair)
        own = jnp.where(core == 0, rows[:, 0], rows[:, 1]).reshape(8 * n, -1)
        far = jnp.where(core == 0, rows[:, 1], rows[:, 0]).reshape(8 * n, -1)
        part = dot(own, cycle_inter, ((1,), (0,))) + dot(far, other, ((1,), (0,)))
        outs[h].append(scatter_sum(part.reshape(4, 2, n, part.shape[1])))
    return jnp.concatenate(outs[0] + outs[1], 0)


def solution(mesh):
    fine = Mesh(mesh.devices.reshape(2, 4, 4, 2, 2), AXES)
    group, shard = ("zl", "x"), ("y", "zh", "c")
    return jax.shard_map(
        shards,
        mesh=fine,
        in_specs=(P(None, shard), P(group, shard), P(shard, group)),
        out_specs=P(shard, group),
        check_vma=False,
    )
```

```python
import functools

import jax
import jax.numpy as jnp
from jax import lax
from jax.experimental import pallas as pl
from jax.experimental.pallas import tpu as pltpu
from jax.sharding import Mesh, PartitionSpec as P

AXES = ("zl", "x", "y", "zh", "c")
C = 256
O = 32
DEPTH = 512
SLOTS = 2
SWAP = ((0, 1), (1, 0))


def halves(x):
    high = x.astype(jnp.bfloat16)
    return high, (x - high.astype(jnp.float32)).astype(jnp.bfloat16)


def product(a, b, dims):
    (a_high, a_low), (b_high, b_low) = a, b
    run = functools.partial(
        lax.dot_general, dimension_numbers=(dims, ((), ())), preferred_element_type=jnp.float32
    )
    return run(a_high, b_high) + run(a_low, b_high) + run(a_high, b_low)


def ladder_kernel(h, core_ref, v_hbm, t_hbm, far_ref, own_ref, t_held, v_held, t_sem, v_sem):
    slots, rows, core = t_held.shape[0], C, core_ref[0]
    steps = t_hbm.shape[1] // DEPTH
    starts = (2 - 2 * core + h, 2 * core + h)

    def copies(k):
        columns, slot = pl.ds(pl.multiple_of(k * DEPTH, DEPTH), DEPTH), lax.rem(k, slots)
        made = [pltpu.make_async_copy(t_hbm.at[:, columns], t_held.at[slot], t_sem.at[slot])]
        for side, start in enumerate(starts):
            made.append(
                pltpu.make_async_copy(
                    v_hbm.at[pl.ds(pl.multiple_of(start * rows, rows), rows), columns],
                    v_held.at[slot, pl.ds(side * rows, rows)],
                    v_sem.at[slot, side],
                )
            )
        return made

    for k in range(slots - 1):
        for copy in copies(jnp.int32(k)):
            copy.start()
    far_ref[...] = jnp.zeros_like(far_ref)
    own_ref[...] = jnp.zeros_like(own_ref)

    def step(k, _):
        for copy in copies(k):
            copy.wait()

        @pl.when(k + slots - 1 < steps)
        def _():
            for copy in copies(k + slots - 1):
                copy.start()

        slot = lax.rem(k, slots)
        part = product(halves(v_held[slot]), halves(t_held[slot]), ((1,), (1,)))
        far_ref[...] += part[:rows]
        own_ref[...] += part[rows:]
        return 0

    lax.fori_loop(0, steps, step, 0)


def ladder(core, integrals, amplitudes, h):
    ef, pairs = integrals.shape[1], amplitudes.shape[0]
    vmem, hbm = pl.BlockSpec(memory_space=pltpu.VMEM), pl.BlockSpec(memory_space=pl.ANY)
    return pl.pallas_call(
        functools.partial(ladder_kernel, h),
        out_shape=[jax.ShapeDtypeStruct((C, pairs), jnp.float32)] * 2,
        in_specs=[pl.BlockSpec(memory_space=pltpu.SMEM), hbm, hbm],
        out_specs=[vmem] * 2,
        scratch_shapes=[
            pltpu.VMEM((SLOTS, pairs, DEPTH), jnp.float32),
            pltpu.VMEM((SLOTS, 2 * C, DEPTH), jnp.float32),
            pltpu.SemaphoreType.DMA((SLOTS,)),
            pltpu.SemaphoreType.DMA((SLOTS, 2)),
        ],
        compiler_params=pltpu.CompilerParams(vmem_limit_bytes=52 * 1024 * 1024),
        cost_estimate=pl.CostEstimate(
            flops=12 * C * pairs * ef,
            bytes_accessed=4 * ef * (2 * C + pairs),
            transcendentals=0,
        ),
    )(core, integrals, amplitudes)


def cycle_kernel(place_ref, own_rows, rows1, rows2, rows3, w_own, w_far, out_ref, *scratch):
    half = w_own.shape[0]

    @pl.when(pl.program_id(0) == 0)
    def _():
        for step, rows in enumerate((own_rows, rows1, rows2, rows3)):
            for other in range(2):
                to = pl.ds(pl.multiple_of(place_ref[2 * step + other] * O, O), O)
                for side in range(2):
                    start = pl.multiple_of(place_ref[8 + side] * half, half)
                    high, low = halves(rows[other, :, pl.ds(start, half)])
                    scratch[2 * side][to, :] = high
                    scratch[2 * side + 1][to, :] = low

    own = (scratch[0][...], scratch[1][...])
    far = (scratch[2][...], scratch[3][...])
    out_ref[...] = product(own, halves(w_own[...]), ((1,), (0,))) + product(
        far, halves(w_far[...]), ((1,), (0,))
    )


def cycle(place, rows, w_own, w_far):
    half, columns = w_own.shape
    wide = 256
    whole = pl.BlockSpec(rows[0].shape, lambda n, place: (0, 0, 0))
    panel = pl.BlockSpec((half, wide), lambda n, place: (0, n))
    return pl.pallas_call(
        cycle_kernel,
        out_shape=jax.ShapeDtypeStruct((8 * O, columns), jnp.float32),
        grid_spec=pltpu.PrefetchScalarGridSpec(
            num_scalar_prefetch=1,
            grid=(columns // wide,),
            in_specs=[whole] * 4 + [panel] * 2,
            out_specs=pl.BlockSpec((8 * O, wide), lambda n, place: (0, n)),
            scratch_shapes=[pltpu.VMEM((8 * O, half), jnp.bfloat16)] * 4,
        ),
        compiler_params=pltpu.CompilerParams(
            dimension_semantics=("arbitrary",), vmem_limit_bytes=24 * 1024 * 1024
        ),
        cost_estimate=pl.CostEstimate(
            flops=6 * 8 * O * 2 * half * columns,
            bytes_accessed=4 * (2 * half * columns + 8 * O * (2 * half + columns)),
            transcendentals=0,
        ),
    )(place, *rows, w_own, w_far)


def regroup_kernel(got_ref, out_ref, held):
    blocks, rows, columns = got_ref.shape
    total = got_ref[0]
    for n in range(1, blocks):
        total = total + got_ref[n]
    for i in range(columns // O):
        held[i] = total[:, i * O : (i + 1) * O]
    for c in range(rows):
        out_ref[:, c * O : (c + 1) * O] = held[:, c, :]


def finish_kernel(done_ref, got_ref, out_ref):
    rows = done_ref.shape[0]
    total = got_ref[0]
    for n in range(1, got_ref.shape[0]):
        total = total + got_ref[n]
    out_ref[:rows, :] = done_ref[...]
    out_ref[rows:, :] = total


def small(kernel, shape, scratch, *args):
    vmem = pl.BlockSpec(memory_space=pltpu.VMEM)
    size = 4 * sum(a.size for a in args)
    return pl.pallas_call(
        kernel,
        out_shape=jax.ShapeDtypeStruct(shape, jnp.float32),
        in_specs=[vmem] * len(args),
        out_specs=vmem,
        scratch_shapes=scratch,
        compiler_params=pltpu.CompilerParams(vmem_limit_bytes=8 * 1024 * 1024),
        cost_estimate=pl.CostEstimate(flops=size, bytes_accessed=size, transcendentals=0),
    )(*args)


def scatter(x):
    return lax.all_to_all(x, ("y", "zh"), 0, 0)


def shards(amplitudes, integrals, cycle_inter):
    core, x, zl = (lax.axis_index(name).astype(jnp.int32) for name in ("c", "x", "zl"))
    place = jnp.stack(
        [(zl + other) % 2 * 4 + (x + 4 - step) % 4 for step in range(4) for other in range(2)]
        + [core, 1 - core]
    )
    other = lax.ppermute(cycle_inter, "c", SWAP)
    near, kept = [], []
    for h in range(2):
        far_block, own_block = ladder(core.reshape(1), integrals, amplitudes, h)
        near.append(lax.ppermute(far_block, "c", SWAP))
        kept.append(own_block)
    got = []
    for h in range(2):
        block = scatter((kept[h] + near[h]).reshape(8, C // 8, O * O))
        mine = small(
            regroup_kernel, (O, C // 8 * O), [pltpu.VMEM((O, C // 8, O), jnp.float32)], block
        )
        far = lax.ppermute(mine, "zl", SWAP)
        pair = jnp.stack([mine, far])
        rows = [pair]
        for step in (1, 2, 3):
            rows.append(lax.ppermute(pair, "x", [(i, (i + step) % 4) for i in range(4)]))
        part = cycle(place, rows, cycle_inter, other)
        got.append(scatter(part.reshape(8, O, part.shape[1])))
    return small(finish_kernel, (2 * O, got[1].shape[2]), [], jnp.sum(got[0], 0), got[1])


def solution(mesh):
    fine = Mesh(mesh.devices.reshape(2, 4, 4, 2, 2), AXES)
    group, shard = ("zl", "x"), ("y", "zh", "c")
    return jax.shard_map(
        shards,
        mesh=fine,
        in_specs=(P(None, shard), P(group, shard), P(shard, group)),
        out_specs=P(shard, group),
        check_vma=False,
    )
```

```python
import functools

import jax
import jax.numpy as jnp
from jax import lax
from jax.experimental import pallas as pl
from jax.experimental.pallas import tpu as pltpu
from jax.sharding import Mesh, PartitionSpec as P

AXES = ("zl", "x", "y", "zh", "c")
C = 256
O = 32
DEPTH = 512
SLOTS = 2
SWAP = ((0, 1), (1, 0))


def halves(x):
    high = x.astype(jnp.bfloat16)
    return high, (x - high.astype(jnp.float32)).astype(jnp.bfloat16)


def product(a, b, dims):
    (a_high, a_low), (b_high, b_low) = a, b
    run = functools.partial(
        lax.dot_general, dimension_numbers=(dims, ((), ())), preferred_element_type=jnp.float32
    )
    return run(a_high, b_high) + run(a_low, b_high) + run(a_high, b_low)


def ladder_kernel(h, core_ref, v_hbm, t_hbm, far_ref, own_ref, t_held, v_held, t_sem, v_sem):
    slots, rows, core = t_held.shape[0], C, core_ref[0]
    steps = t_hbm.shape[1] // DEPTH
    starts = (2 - 2 * core + h, 2 * core + h)

    def copies(k):
        columns, slot = pl.ds(pl.multiple_of(k * DEPTH, DEPTH), DEPTH), lax.rem(k, slots)
        made = [pltpu.make_async_copy(t_hbm.at[:, columns], t_held.at[slot], t_sem.at[slot])]
        for side, start in enumerate(starts):
            made.append(
                pltpu.make_async_copy(
                    v_hbm.at[pl.ds(pl.multiple_of(start * rows, rows), rows), columns],
                    v_held.at[slot, pl.ds(side * rows, rows)],
                    v_sem.at[slot, side],
                )
            )
        return made

    for k in range(slots - 1):
        for copy in copies(jnp.int32(k)):
            copy.start()
    far_ref[...] = jnp.zeros_like(far_ref)
    own_ref[...] = jnp.zeros_like(own_ref)

    def step(k, _):
        for copy in copies(k):
            copy.wait()

        @pl.when(k + slots - 1 < steps)
        def _():
            for copy in copies(k + slots - 1):
                copy.start()

        slot = lax.rem(k, slots)
        part = product(halves(v_held[slot]), halves(t_held[slot]), ((1,), (1,)))
        far_ref[...] += part[:rows]
        own_ref[...] += part[rows:]
        return 0

    lax.fori_loop(0, steps, step, 0)


def ladder(core, integrals, amplitudes, h):
    ef, pairs = integrals.shape[1], amplitudes.shape[0]
    vmem, hbm = pl.BlockSpec(memory_space=pltpu.VMEM), pl.BlockSpec(memory_space=pl.ANY)
    return pl.pallas_call(
        functools.partial(ladder_kernel, h),
        out_shape=[jax.ShapeDtypeStruct((C, pairs), jnp.float32)] * 2,
        in_specs=[pl.BlockSpec(memory_space=pltpu.SMEM), hbm, hbm],
        out_specs=[vmem] * 2,
        scratch_shapes=[
            pltpu.VMEM((SLOTS, pairs, DEPTH), jnp.float32),
            pltpu.VMEM((SLOTS, 2 * C, DEPTH), jnp.float32),
            pltpu.SemaphoreType.DMA((SLOTS,)),
            pltpu.SemaphoreType.DMA((SLOTS, 2)),
        ],
        compiler_params=pltpu.CompilerParams(vmem_limit_bytes=52 * 1024 * 1024),
        cost_estimate=pl.CostEstimate(
            flops=12 * C * pairs * ef,
            bytes_accessed=4 * ef * (2 * C + pairs),
            transcendentals=0,
        ),
    )(core, integrals, amplitudes)


def cycle_kernel(place_ref, *refs):
    rows, (w_own, w_far, out_ref), scratch = refs[:8], refs[8:11], refs[11:]
    half = w_own.shape[0]

    @pl.when(pl.program_id(0) == 0)
    def _():
        for n, block in enumerate(rows):
            to = pl.ds(pl.multiple_of(place_ref[n] * O, O), O)
            for side in range(2):
                start = pl.multiple_of(place_ref[8 + side] * half, half)
                high, low = halves(block[:, pl.ds(start, half)])
                scratch[2 * side][to, :] = high
                scratch[2 * side + 1][to, :] = low

    own = (scratch[0][...], scratch[1][...])
    far = (scratch[2][...], scratch[3][...])
    out_ref[...] = product(own, halves(w_own[...]), ((1,), (0,))) + product(
        far, halves(w_far[...]), ((1,), (0,))
    )


def cycle(place, rows, w_own, w_far):
    half, columns = w_own.shape
    wide = 512
    whole = pl.BlockSpec(rows[0].shape, lambda n, place: (0, 0))
    panel = pl.BlockSpec((half, wide), lambda n, place: (0, n))
    return pl.pallas_call(
        cycle_kernel,
        out_shape=jax.ShapeDtypeStruct((8 * O, columns), jnp.float32),
        grid_spec=pltpu.PrefetchScalarGridSpec(
            num_scalar_prefetch=1,
            grid=(columns // wide,),
            in_specs=[whole] * 8 + [panel] * 2,
            out_specs=pl.BlockSpec((8 * O, wide), lambda n, place: (0, n)),
            scratch_shapes=[pltpu.VMEM((8 * O, half), jnp.bfloat16)] * 4,
        ),
        compiler_params=pltpu.CompilerParams(
            dimension_semantics=("arbitrary",), vmem_limit_bytes=24 * 1024 * 1024
        ),
        cost_estimate=pl.CostEstimate(
            flops=6 * 8 * O * 2 * half * columns,
            bytes_accessed=4 * (2 * half * columns + 8 * O * (2 * half + columns)),
            transcendentals=0,
        ),
    )(place, *rows, w_own, w_far)


def regroup_kernel(got_ref, out_ref, held):
    blocks, rows, columns = got_ref.shape
    total = got_ref[0]
    for n in range(1, blocks):
        total = total + got_ref[n]
    for i in range(columns // O):
        held[i] = total[:, i * O : (i + 1) * O]
    for c in range(rows):
        out_ref[:, c * O : (c + 1) * O] = held[:, c, :]


def finish_kernel(done_ref, got_ref, out_ref):
    rows = done_ref.shape[0]
    total = got_ref[0]
    for n in range(1, got_ref.shape[0]):
        total = total + got_ref[n]
    out_ref[:rows, :] = done_ref[...]
    out_ref[rows:, :] = total


def small(kernel, shape, scratch, *args):
    vmem = pl.BlockSpec(memory_space=pltpu.VMEM)
    size = 4 * sum(a.size for a in args)
    return pl.pallas_call(
        kernel,
        out_shape=jax.ShapeDtypeStruct(shape, jnp.float32),
        in_specs=[vmem] * len(args),
        out_specs=vmem,
        scratch_shapes=scratch,
        compiler_params=pltpu.CompilerParams(vmem_limit_bytes=8 * 1024 * 1024),
        cost_estimate=pl.CostEstimate(flops=size, bytes_accessed=size, transcendentals=0),
    )(*args)


def scatter(x):
    return lax.all_to_all(x, ("y", "zh"), 0, 0)


def shards(amplitudes, integrals, cycle_inter):
    core, x, zl = (lax.axis_index(name).astype(jnp.int32) for name in ("c", "x", "zl"))
    place = jnp.stack(
        [(zl + other) % 2 * 4 + (x + 4 - step) % 4 for other in range(2) for step in range(4)]
        + [core, 1 - core]
    )
    other = lax.ppermute(cycle_inter, "c", SWAP)
    near, kept = [], []
    for h in range(2):
        far_block, own_block = ladder(core.reshape(1), integrals, amplitudes, h)
        near.append(lax.ppermute(far_block, "c", SWAP))
        kept.append(own_block)
    got = []
    for h in range(2):
        block = scatter((kept[h] + near[h]).reshape(8, C // 8, O * O))
        mine = small(
            regroup_kernel, (O, C // 8 * O), [pltpu.VMEM((O, C // 8, O), jnp.float32)], block
        )
        far = lax.ppermute(mine, "zl", SWAP)
        rows = []
        for block in (mine, far):
            rows.append(block)
            for step in (1, 2, 3):
                rows.append(lax.ppermute(block, "x", [(i, (i + step) % 4) for i in range(4)]))
        part = cycle(place, rows, cycle_inter, other)
        got.append(scatter(part.reshape(8, O, part.shape[1])))
    return small(finish_kernel, (2 * O, got[1].shape[2]), [], jnp.sum(got[0], 0), got[1])


def solution(mesh):
    fine = Mesh(mesh.devices.reshape(2, 4, 4, 2, 2), AXES)
    group, shard = ("zl", "x"), ("y", "zh", "c")
    return jax.shard_map(
        shards,
        mesh=fine,
        in_specs=(P(None, shard), P(group, shard), P(shard, group)),
        out_specs=P(shard, group),
        check_vma=False,
    )
```

```python
import functools

import jax
import jax.numpy as jnp
from jax import lax
from jax.experimental import pallas as pl
from jax.experimental.pallas import tpu as pltpu
from jax.sharding import Mesh, PartitionSpec as P

AXES = ("zl", "x", "y", "zh", "c")
C = 256
O = 32
DEPTH = 512
SLOTS = 2
SWAP = ((0, 1), (1, 0))


def halves(x):
    high = x.astype(jnp.bfloat16)
    return high, (x - high.astype(jnp.float32)).astype(jnp.bfloat16)


def product(a, b, dims):
    (a_high, a_low), (b_high, b_low) = a, b
    run = functools.partial(
        lax.dot_general, dimension_numbers=(dims, ((), ())), preferred_element_type=jnp.float32
    )
    return run(a_high, b_high) + run(a_low, b_high) + run(a_high, b_low)


def ladder_kernel(h, core_ref, v_hbm, t_hbm, far_ref, own_ref, t_held, v_held, t_sem, v_sem):
    slots, rows, core = t_held.shape[0], C, core_ref[0]
    steps = t_hbm.shape[1] // DEPTH
    starts = (2 - 2 * core + h, 2 * core + h)

    def copies(k):
        columns, slot = pl.ds(pl.multiple_of(k * DEPTH, DEPTH), DEPTH), lax.rem(k, slots)
        made = [pltpu.make_async_copy(t_hbm.at[:, columns], t_held.at[slot], t_sem.at[slot])]
        for side, start in enumerate(starts):
            made.append(
                pltpu.make_async_copy(
                    v_hbm.at[pl.ds(pl.multiple_of(start * rows, rows), rows), columns],
                    v_held.at[slot, pl.ds(side * rows, rows)],
                    v_sem.at[slot, side],
                )
            )
        return made

    for k in range(slots - 1):
        for copy in copies(jnp.int32(k)):
            copy.start()
    far_ref[...] = jnp.zeros_like(far_ref)
    own_ref[...] = jnp.zeros_like(own_ref)

    def step(k, _):
        for copy in copies(k):
            copy.wait()

        @pl.when(k + slots - 1 < steps)
        def _():
            for copy in copies(k + slots - 1):
                copy.start()

        slot = lax.rem(k, slots)
        part = product(halves(v_held[slot]), halves(t_held[slot]), ((1,), (1,)))
        far_ref[...] += part[:rows]
        own_ref[...] += part[rows:]
        return 0

    lax.fori_loop(0, steps, step, 0)


def ladder(core, integrals, amplitudes, h):
    ef, pairs = integrals.shape[1], amplitudes.shape[0]
    vmem, hbm = pl.BlockSpec(memory_space=pltpu.VMEM), pl.BlockSpec(memory_space=pl.ANY)
    return pl.pallas_call(
        functools.partial(ladder_kernel, h),
        out_shape=[jax.ShapeDtypeStruct((C, pairs), jnp.float32)] * 2,
        in_specs=[pl.BlockSpec(memory_space=pltpu.SMEM), hbm, hbm],
        out_specs=[vmem] * 2,
        scratch_shapes=[
            pltpu.VMEM((SLOTS, pairs, DEPTH), jnp.float32),
            pltpu.VMEM((SLOTS, 2 * C, DEPTH), jnp.float32),
            pltpu.SemaphoreType.DMA((SLOTS,)),
            pltpu.SemaphoreType.DMA((SLOTS, 2)),
        ],
        compiler_params=pltpu.CompilerParams(vmem_limit_bytes=52 * 1024 * 1024),
        cost_estimate=pl.CostEstimate(
            flops=12 * C * pairs * ef,
            bytes_accessed=4 * ef * (2 * C + pairs),
            transcendentals=0,
        ),
    )(core, integrals, amplitudes)


def cycle_kernel(place_ref, *refs):
    rows, w, out_ref, scratch = refs[:8], refs[8:12], refs[12], refs[13:]
    half = w[0].shape[0]

    @pl.when(pl.program_id(0) == 0)
    def _():
        for n, block in enumerate(rows):
            to = pl.ds(pl.multiple_of(place_ref[n] * O, O), O)
            for side in range(2):
                start = pl.multiple_of(place_ref[8 + side] * half, half)
                high, low = halves(block[:, pl.ds(start, half)])
                scratch[2 * side][to, :] = high
                scratch[2 * side + 1][to, :] = low

    own = (scratch[0][...], scratch[1][...])
    far = (scratch[2][...], scratch[3][...])
    out_ref[...] = product(own, (w[0][...], w[1][...]), ((1,), (0,))) + product(
        far, (w[2][...], w[3][...]), ((1,), (0,))
    )


def split_kernel(own_ref, far_ref, *outs):
    outs[0][...], outs[1][...] = halves(own_ref[...])
    outs[2][...], outs[3][...] = halves(far_ref[...])


def split_w(own, far):
    half, columns = own.shape
    panel = pl.BlockSpec((half, 256), lambda n: (0, n))
    return pl.pallas_call(
        split_kernel,
        out_shape=[jax.ShapeDtypeStruct(own.shape, jnp.bfloat16)] * 4,
        grid=(columns // 256,),
        in_specs=[panel] * 2,
        out_specs=[panel] * 4,
        compiler_params=pltpu.CompilerParams(
            dimension_semantics=("arbitrary",), vmem_limit_bytes=16 * 1024 * 1024
        ),
        cost_estimate=pl.CostEstimate(
            flops=4 * own.size, bytes_accessed=16 * own.size, transcendentals=0
        ),
        name="split_w",
    )(own, far)


def cycle(place, rows, w):
    half, columns = w[0].shape
    wide = 512
    whole = pl.BlockSpec(rows[0].shape, lambda n, place: (0, 0))
    panel = pl.BlockSpec((half, wide), lambda n, place: (0, n))
    return pl.pallas_call(
        cycle_kernel,
        out_shape=jax.ShapeDtypeStruct((8 * O, columns), jnp.float32),
        grid_spec=pltpu.PrefetchScalarGridSpec(
            num_scalar_prefetch=1,
            grid=(columns // wide,),
            in_specs=[whole] * 8 + [panel] * 4,
            out_specs=pl.BlockSpec((8 * O, wide), lambda n, place: (0, n)),
            scratch_shapes=[pltpu.VMEM((8 * O, half), jnp.bfloat16)] * 4,
        ),
        compiler_params=pltpu.CompilerParams(
            dimension_semantics=("arbitrary",), vmem_limit_bytes=24 * 1024 * 1024
        ),
        cost_estimate=pl.CostEstimate(
            flops=6 * 8 * O * 2 * half * columns,
            bytes_accessed=4 * (2 * half * columns + 8 * O * (2 * half + columns)),
            transcendentals=0,
        ),
    )(place, *rows, *w)


def regroup_kernel(got_ref, out_ref, held):
    blocks, rows, columns = got_ref.shape
    total = got_ref[0]
    for n in range(1, blocks):
        total = total + got_ref[n]
    for i in range(columns // O):
        held[i] = total[:, i * O : (i + 1) * O]
    for c in range(rows):
        out_ref[:, c * O : (c + 1) * O] = held[:, c, :]


def finish_kernel(done_ref, got_ref, out_ref):
    rows = done_ref.shape[0]
    total = got_ref[0]
    for n in range(1, got_ref.shape[0]):
        total = total + got_ref[n]
    out_ref[:rows, :] = done_ref[...]
    out_ref[rows:, :] = total


def small(kernel, shape, scratch, *args):
    vmem = pl.BlockSpec(memory_space=pltpu.VMEM)
    size = 4 * sum(a.size for a in args)
    return pl.pallas_call(
        kernel,
        out_shape=jax.ShapeDtypeStruct(shape, jnp.float32),
        in_specs=[vmem] * len(args),
        out_specs=vmem,
        scratch_shapes=scratch,
        compiler_params=pltpu.CompilerParams(vmem_limit_bytes=8 * 1024 * 1024),
        cost_estimate=pl.CostEstimate(flops=size, bytes_accessed=size, transcendentals=0),
    )(*args)


def scatter(x):
    return lax.all_to_all(x, ("y", "zh"), 0, 0)


def shards(amplitudes, integrals, cycle_inter):
    core, x, zl = (lax.axis_index(name).astype(jnp.int32) for name in ("c", "x", "zl"))
    place = jnp.stack(
        [(zl + other) % 2 * 4 + (x + 4 - step) % 4 for other in range(2) for step in range(4)]
        + [core, 1 - core]
    )
    other = lax.ppermute(cycle_inter, "c", SWAP)
    parts = split_w(cycle_inter, other)
    near, kept = [], []
    for h in range(2):
        far_block, own_block = ladder(core.reshape(1), integrals, amplitudes, h)
        near.append(lax.ppermute(far_block, "c", SWAP))
        kept.append(own_block)
    got = []
    for h in range(2):
        block = scatter((kept[h] + near[h]).reshape(8, C // 8, O * O))
        mine = small(
            regroup_kernel, (O, C // 8 * O), [pltpu.VMEM((O, C // 8, O), jnp.float32)], block
        )
        far = lax.ppermute(mine, "zl", SWAP)
        rows = []
        for block in (mine, far):
            rows.append(block)
            for step in (1, 2, 3):
                rows.append(lax.ppermute(block, "x", [(i, (i + step) % 4) for i in range(4)]))
        part = cycle(place, rows, parts)
        got.append(scatter(part.reshape(8, O, part.shape[1])))
    return small(finish_kernel, (2 * O, got[1].shape[2]), [], jnp.sum(got[0], 0), got[1])


def solution(mesh):
    fine = Mesh(mesh.devices.reshape(2, 4, 4, 2, 2), AXES)
    group, shard = ("zl", "x"), ("y", "zh", "c")
    return jax.shard_map(
        shards,
        mesh=fine,
        in_specs=(P(None, shard), P(group, shard), P(shard, group)),
        out_specs=P(shard, group),
        check_vma=False,
    )
```
